256 devices in a mesh: ctx: 16 (over x_hi, y, core), head: 16 (over z, x_lo).
Axes of the slice: x: 4 (x_hi: 2, x_lo: 2; x = x_hi * 2 + x_lo), y: 4, z: 8, core: 2. Of those that a mesh axis runs over, the one named last changes fastest.
Arguments:
- queries: bfloat16 [32, 32768, 128], P('head', 'ctx'), may hold values from -6 to 6
- key_states: bfloat16 [16, 32768, 128], P('head', 'ctx'), may hold values from -6 to 6
- value_states: bfloat16 [16, 32768, 128], P('head', 'ctx'), may hold values from -6 to 6
- attn_output: bfloat16 [32768, 4096], P(('ctx', 'head')), may hold values from -6 to 6
- out_cotangent: bfloat16 [32768, 4096], P(('ctx', 'head')), may hold values from -6 to 6
- logsumexp: float32 [32, 32768], P('head', 'ctx'), may hold values from 4.5 to 6.5
- doc_start: int32 [32768], P('ctx'), may hold values from 0 to 31744, as said below
Outputs:
- grad_queries: bfloat16 [32, 32768, 128], P('head', 'ctx')
- grad_keys: bfloat16 [16, 32768, 128], P('head', 'ctx')
- grad_values: bfloat16 [16, 32768, 128], P('head', 'ctx')
The draws below stay inside these ranges and needn't reach their ends.
Inputs may be any that keep to these rules, and one draw needn't show every extreme that they name: doc_start[t] <= t and never falls; each value is the first position of a document; doc_start[0] = 0; the last 1024 positions form one document that starts at 31744; every other document has half of 1024 to 3072 tokens, except that the one just before the last may be shorter.
All inputs are finite; a program needn't handle non-finite values.
Results may differ from the reference program's by a relative error of at most 0.0049.
Values may be sent and summed in bfloat16 or wider, within the bound.
A program may use at most 64 MiB of HBM per device.

```python
import jax
import jax.numpy as jnp
from jax import lax

HQ = 32
KV = 16
HD = 128
W = 1024
QPRE = 168
TOK_DEV = 2048
TOKENS = 32768


def draw_doc_start(key, part):
    lowest = max(W // 2, 1)
    highest = 3 * W + 1
    doc_count = TOKENS // lowest + 2
    lengths = jax.random.randint(key, (doc_count,), lowest, highest, dtype=jnp.int32)
    doc_ends = jnp.cumsum(lengths).astype(jnp.int32)
    starts = jnp.concatenate([jnp.zeros((1,), jnp.int32), doc_ends[:-1]])
    positions = jnp.arange(TOKENS, dtype=jnp.int32)
    owner_index = (jnp.searchsorted(starts, positions, side='right') - 1).astype(jnp.int32)
    drawn = starts[owner_index].astype(jnp.int32)
    last_start = jnp.int32(TOKENS - W)
    return jnp.where(positions >= last_start, last_start, drawn).astype(jnp.int32)


def block_levels(rng, dims, split, low, high):
    factor_of = 1.0
    for dim, blocks in split:
        steps = jax.random.uniform(jax.random.fold_in(jax.random.fold_in(rng, 6), dim), (blocks,), jnp.float32, low / len(split), high / len(split))
        factor_of = factor_of * jnp.repeat(jnp.exp(steps), dims[dim] // blocks).reshape((-1,) + (1,) * (len(dims) - 1 - dim))
    return factor_of


def gaussian(rng, shape, deviation, most, cuts=(), kind=jnp.bfloat16):
    factor_of = block_levels(rng, shape, cuts, -0.22, 0.18) if cuts else 1.0
    array = jax.random.normal(rng, shape, jnp.float32) * deviation * factor_of
    return jnp.minimum(jnp.maximum(array, -most), most).astype(kind)


def setup_inputs(seed: int = 0) -> dict:
    key_list = jax.random.split(jax.random.key(seed), 8)
    queries = gaussian(key_list[0], (HQ, TOKENS, HD), 1.0, 6.0, ((0, 16), (1, 16)))
    key_states = gaussian(key_list[1], (KV, TOKENS, HD), 1.0, 6.0, ((0, 16), (1, 16)))
    value_states = gaussian(key_list[2], (KV, TOKENS, HD), 1.0, 6.0, ((0, 16), (1, 16)))
    attn_output = gaussian(key_list[3], (TOKENS, HQ * HD), 1.0, 6.0, ((0, 256),))
    out_cotangent = gaussian(key_list[4], (TOKENS, HQ * HD), 1.0, 6.0, ((0, 256),))
    logsumexp = jnp.clip(4.5 + 2.0 * jax.random.uniform(key_list[5], (HQ, TOKENS), jnp.float32) ** block_levels(key_list[5], (HQ, TOKENS), ((0, 16), (1, 16)), -0.2, 0.2), 4.5, 6.5)
    doc_start = draw_doc_start(jax.random.fold_in(key_list[7], 71), 0)
    return {"queries": queries, "key_states": key_states, "value_states": value_states, "attn_output": attn_output, "out_cotangent": out_cotangent, "logsumexp": logsumexp, "doc_start": doc_start}


def band_tile(query_block, cotan_block, lse_block, delta_block, key_block, value_block, allowed, score_scale):
    f32 = jnp.float32
    scores = jnp.einsum("kgrd,kjd->kgrj", query_block.astype(f32), key_block.astype(f32)) * score_scale
    probs = jnp.where(allowed, jnp.exp(scores - lse_block[..., None]), jnp.float32(0.0))
    probs_low = probs.astype(jnp.bfloat16)
    dprobs = jnp.einsum("rkgd,kjd->kgrj", cotan_block.astype(f32), value_block.astype(f32))
    dscores = (probs * (dprobs - delta_block[..., None])).astype(jnp.bfloat16)
    grad_value = jnp.einsum("kgrj,rkgd->kjd", probs_low.astype(f32), cotan_block.astype(f32))
    grad_key = jnp.einsum("kgrj,kgrd->kjd", dscores.astype(f32), query_block.astype(f32)) * score_scale
    grad_query = jnp.einsum("kgrj,kjd->kgrd", dscores.astype(f32), key_block.astype(f32)) * score_scale
    return grad_query, grad_key, grad_value


def reference(queries, key_states, value_states, attn_output, out_cotangent, logsumexp, doc_start):
    kv_heads = key_states.shape[0]
    total = key_states.shape[1]
    head_dim = key_states.shape[2]
    groups = HQ // KV
    window = W
    block_rows = min(512, TOK_DEV)
    n_blocks = total // block_rows
    span = block_rows + window
    score_scale = QPRE ** -0.5
    cotangent = out_cotangent.reshape(total, HQ, head_dim)
    output = attn_output.reshape(total, HQ, head_dim)
    row_delta = jnp.sum(cotangent.astype(jnp.float32) * output.astype(jnp.float32), axis=2)
    delta_grouped = row_delta.reshape(total, kv_heads, groups).transpose(1, 2, 0)
    lse_grouped = logsumexp.reshape(kv_heads, groups, total)
    query_grouped = queries.reshape(kv_heads, groups, total, head_dim)
    padding = jnp.zeros((kv_heads, window, head_dim), jnp.bfloat16)
    key_ext = jnp.concatenate([padding, key_states], axis=1)
    value_ext = jnp.concatenate([padding, value_states], axis=1)
    row_iota = jnp.arange(block_rows, dtype=jnp.int32)
    col_iota = jnp.arange(span, dtype=jnp.int32)
    distance = row_iota[:, None] + window - col_iota[None, :]
    near = (distance >= 0) & (distance < window)

    def block_step(index, carry):
        grad_key_ext, grad_value_ext, grad_query_all = carry
        first = (index * block_rows).astype(jnp.int32)
        query_block = lax.dynamic_slice_in_dim(query_grouped, first, block_rows, 2)
        lse_block = lax.dynamic_slice_in_dim(lse_grouped, first, block_rows, 2)
        delta_block = lax.dynamic_slice_in_dim(delta_grouped, first, block_rows, 2)
        cotan_block = lax.dynamic_slice_in_dim(cotangent, first, block_rows, 0).reshape(block_rows, kv_heads, groups, head_dim)
        key_block = lax.dynamic_slice_in_dim(key_ext, first, span, 1)
        value_block = lax.dynamic_slice_in_dim(value_ext, first, span, 1)
        start_rel = lax.dynamic_slice_in_dim(doc_start, first, block_rows, 0)
        key_local = first - window + col_iota
        allowed = near & (key_local[None, :] >= start_rel[:, None])
        grad_query, grad_key, grad_value = band_tile(query_block, cotan_block, lse_block, delta_block, key_block, value_block, allowed, score_scale)
        grad_key_ext = lax.dynamic_update_slice_in_dim(grad_key_ext, lax.dynamic_slice_in_dim(grad_key_ext, first, span, 1) + grad_key, first, 1)
        grad_value_ext = lax.dynamic_update_slice_in_dim(grad_value_ext, lax.dynamic_slice_in_dim(grad_value_ext, first, span, 1) + grad_value, first, 1)
        grad_query_all = lax.dynamic_update_slice_in_dim(grad_query_all, grad_query.astype(jnp.bfloat16), first, 2)
        return grad_key_ext, grad_value_ext, grad_query_all

    initial = (jnp.zeros((kv_heads, total + window, head_dim), jnp.float32),
               jnp.zeros((kv_heads, total + window, head_dim), jnp.float32),
               jnp.zeros((kv_heads, groups, total, head_dim), jnp.bfloat16))
    grad_key_ext, grad_value_ext, grad_query_all = lax.fori_loop(0, n_blocks, block_step, initial)
    grad_queries = grad_query_all.reshape(HQ, total, head_dim)
    grad_keys = grad_key_ext[:, window:].astype(jnp.bfloat16)
    grad_values = grad_value_ext[:, window:].astype(jnp.bfloat16)
    return (grad_queries, grad_keys, grad_values)
```

```python
import functools

import jax
import jax.numpy as jnp
from jax import lax
from jax.experimental import pallas as pl
from jax.experimental.pallas import tpu as pltpu
from jax.sharding import PartitionSpec as P

W = 1024
QPRE = 168
SCALE = QPRE ** (-0.5)
LOG2E = 1.4426950408889634
MESH = pl.DeviceIdType.MESH
BF = jnp.bfloat16
F32 = jnp.float32
NT = (((1,), (1,)), ((), ()))
NN = (((1,), (0,)), ((), ()))
PEERS = ((0, 1), (1, 0), (7, 0), (1, 1), (7, 1), (2, 0), (6, 0), (2, 1), (6, 1), (3, 0), (5, 0), (3, 1), (5, 1), (4, 0), (4, 1))


def mm(a, b, dims):
    return lax.dot_general(a, b, dims, preferred_element_type=F32)


def side(parts, axis):
    return parts[0] if len(parts) == 1 else jnp.concatenate(parts, axis=axis)


def segments(rows):
    if rows > 1152:
        return ((0, 128, "A"), (128, 1024, "AB"), (1152, 128, "B"))
    return ((0, 128, "A"), (128, rows - 128, "AB"))


def attention_kernel(
    q_hbm, k_hbm, v_hbm, out_hbm, cot_hbm, lse_hbm, doc_hbm,
    dq_hbm, dk_hbm, dv_hbm,
    qv, kx, vx, kt, outv, cotv, lsev, docv, cots, dels, delsrc, probs, dka, dva, dqo, dko, dvo,
    load_sem, halo_send, halo_recv, cot_send, cot_recv, del_send, del_recv,
    fwd_send, fwd_recv, fwd_del_send, fwd_del_recv, store_sem,
):
    ctx = lax.axis_index("ctx")
    head = lax.axis_index("head")
    z, x = head // 2, head % 2
    nxt, prv = lax.rem(ctx + 1, 16), lax.rem(ctx + 15, 16)
    peers = [lax.rem(z + dz, 8) * 2 + lax.rem(x + dx, 2) for dz, dx in PEERS]

    barrier = pltpu.get_barrier_semaphore()
    for peer in peers:
        pl.semaphore_signal(barrier, inc=1, device_id={"head": peer}, device_id_type=MESH)
    for peer in (nxt, prv):
        pl.semaphore_signal(barrier, inc=1, device_id={"ctx": peer}, device_id_type=MESH)

    loads = [
        pltpu.make_async_copy(cot_hbm, cotv, load_sem.at[0]),
        pltpu.make_async_copy(out_hbm, outv, load_sem.at[1]),
        pltpu.make_async_copy(q_hbm, qv.at[:, pl.ds(0, 2048), :], load_sem.at[2]),
        pltpu.make_async_copy(k_hbm.at[0], kx.at[pl.ds(1024, 2048), :], load_sem.at[3]),
        pltpu.make_async_copy(v_hbm.at[0], vx.at[pl.ds(1024, 2048), :], load_sem.at[4]),
        pltpu.make_async_copy(lse_hbm, lsev.at[:, pl.ds(0, 2048)], load_sem.at[5]),
        pltpu.make_async_copy(doc_hbm, docv.at[pl.ds(0, 16), :], load_sem.at[6]),
    ]
    for load in loads:
        load.start()

    loads[0].wait()
    loads[1].wait()
    lane = lax.broadcasted_iota(jnp.int32, (128, 128), 1)
    rows_delta = jnp.zeros((128, 128), F32)
    for h in range(32):
        cols = slice(h * 128, (h + 1) * 128)
        product = cotv[:, cols].astype(F32) * outv[:, cols].astype(F32)
        rows_delta = jnp.where(lane == h, jnp.sum(product, axis=1, keepdims=True), rows_delta)
    rows_delta = rows_delta.T
    for j in range(16):
        delsrc[j] = rows_delta[2 * j : 2 * j + 2]

    pl.semaphore_wait(barrier, 17)
    sends = []

    def send(src, dst, send_sem, recv_sem, where):
        copy = pltpu.make_async_remote_copy(
            src_ref=src, dst_ref=dst, send_sem=send_sem, recv_sem=recv_sem, device_id=where, device_id_type=MESH
        )
        copy.start()
        sends.append(copy)

    for n, peer in enumerate(peers):
        send(delsrc.at[peer], dels.at[head], del_send.at[n], del_recv.at[head], {"head": peer})
    for n, peer in enumerate(peers):
        cols = pl.ds(pl.multiple_of(peer * 256, 256), 256)
        send(cotv.at[:, cols], cots.at[head], cot_send.at[n], cot_recv.at[head], {"head": peer})
        if n == 4:
            half = pl.ds(1024, 1024)
            send(k_hbm.at[0, half, :], kx.at[pl.ds(0, 1024), :], halo_send.at[0], halo_recv.at[0], {"ctx": nxt})
            send(v_hbm.at[0, half, :], vx.at[pl.ds(0, 1024), :], halo_send.at[1], halo_recv.at[1], {"ctx": nxt})
            first, past = pl.ds(0, 1024), pl.ds(2048, 1024)
            send(lse_hbm.at[:, first], lsev.at[:, past], halo_send.at[2], halo_recv.at[2], {"ctx": prv})
            send(doc_hbm.at[pl.ds(0, 8), :], docv.at[pl.ds(16, 8), :], halo_send.at[3], halo_recv.at[3], {"ctx": prv})
            send(q_hbm.at[:, first, :], qv.at[:, past, :], halo_send.at[4], halo_recv.at[4], {"ctx": prv})

    cots[head] = cotv[:, pl.ds(pl.multiple_of(head * 256, 256), 256)]
    dels[head] = delsrc[head]
    dka[...] = jnp.zeros_like(dka)
    dva[...] = jnp.zeros_like(dva)

    def waiting(dst, recv_sem, where):
        pltpu.make_async_remote_copy(
            src_ref=dst, dst_ref=dst, send_sem=cot_send.at[0], recv_sem=recv_sem, device_id=where, device_id_type=MESH
        ).wait_recv()

    base = ctx * 2048
    col = lax.broadcasted_iota(jnp.int32, (1, 128), 1)

    def queries_of(q0):
        return jnp.concatenate([qv[0, pl.ds(q0, 128), :], qv[1, pl.ds(q0, 128), :]], axis=0)

    def make_probs(pair, rows, far):
        for which in range(2):
            chunk = pair * 2 + which
            q0 = pl.multiple_of(chunk * 128, 128)
            query = queries_of(q0)
            at = pl.ds(q0, 128)
            lse = jnp.concatenate([lsev[0:1, at], lsev[1:2, at]], axis=1) * LOG2E
            low = jnp.maximum(docv[pl.ds(chunk, 1), :] - base + (W - q0), col + 1) + far
            low = jnp.concatenate([low, low], axis=1)
            high = jnp.concatenate([col, col], axis=1) + W
            span = min(1152, rows - 128 * which)
            for first, count in ((0, min(span, 1024)), (1024, span - 1024)):
                if count <= 0:
                    continue
                scores = mm(kx[pl.ds(q0 + first, count), :], query, NT)
                row = lax.broadcasted_iota(jnp.int32, (count, 256), 0) + first
                allowed = row >= low
                if first == 1024:
                    allowed = allowed & (row <= high)
                value = jnp.where(allowed, jnp.exp2(scores * (SCALE * LOG2E) - lse), 0.0)
                probs[pair, pl.ds(128 * which + first, count), pl.ds(256 * which, 256)] = value

    def use_pair(pair, rows, with_queries):
        q0 = pl.multiple_of(pair * 256, 256)
        query, cot, delta, grads = [], [], [], [[], []]
        for which in range(2):
            chunk = pair * 2 + which
            query.append(queries_of(q0 + 128 * which))
            block = cots[chunk]
            cot.append(jnp.concatenate([block[:, :128], block[:, 128:]], axis=0))
            both = dels[chunk]
            delta.append(jnp.concatenate([both[0:1], both[1:2]], axis=1))
        for first, count, whom in segments(rows):
            at = pl.ds(q0 + first, count)
            used = [w for w in range(2) if "AB"[w] in whom]
            low_probs, low_scores = [], []
            for w in used:
                prob = probs[pair, pl.ds(first, count), pl.ds(256 * w, 256)]
                dprobs = mm(vx[at, :], cot[w], NT)
                dscores = (prob * (dprobs - delta[w])).astype(BF)
                low_probs.append(prob.astype(BF))
                low_scores.append(dscores)
                if with_queries:
                    grads[w].append(mm(kt[:, at], dscores, NN))
            dva[at, :] += mm(side(low_probs, 1), side([cot[w] for w in used], 0), NN)
            dka[at, :] += mm(side(low_scores, 1), side([query[w] for w in used], 0), NN)
        if with_queries:
            for w in range(2):
                total = functools.reduce(jnp.add, grads[w]).T
                total = (total * SCALE).astype(BF)
                at = pl.ds(q0 + 128 * w, 128)
                dqo[0, at, :] = total[:128]
                dqo[1, at, :] = total[128:]

    for load in loads[2:]:
        load.wait()
    for b in range(8, 24):
        kt[:, b * 128 : (b + 1) * 128] = kx[pl.ds(b * 128, 128), :].T

    @pl.loop(4, 8)
    def _(pair):
        make_probs(pair, 1280, 0)

    to_next, to_prev = {"ctx": nxt}, {"ctx": prv}
    waiting(kx.at[pl.ds(0, 1024), :], halo_recv.at[0], to_next)
    for b in range(8):
        kt[:, b * 128 : (b + 1) * 128] = kx[pl.ds(b * 128, 128), :].T

    @pl.loop(0, 4)
    def _(pair):
        make_probs(pair, 1280, 0)

    waiting(lsev.at[:, pl.ds(2048, 1024)], halo_recv.at[2], to_prev)
    waiting(docv.at[pl.ds(16, 8), :], halo_recv.at[3], to_prev)
    waiting(qv.at[:, pl.ds(2048, 1024), :], halo_recv.at[4], to_prev)
    beyond = jnp.where(ctx == 15, 1 << 20, 0)
    for k in range(4):
        make_probs(8 + k, 1024 - 256 * k, beyond)
    waiting(vx.at[pl.ds(0, 1024), :], halo_recv.at[1], to_next)

    def source(step):
        far = (step + 1) // 2
        return lax.rem(z + jnp.where(step % 2 == 1, 8 - far, far), 8)

    def forward(pair, start):
        two = pl.ds(pair * 2, 2)
        past = pl.ds(16 + pair * 2, 2)
        for src, dst, ssem, rsem in (
            (dels.at[two], dels.at[past], fwd_del_send.at[pair], fwd_del_recv.at[pair]),
            (cots.at[two], cots.at[past], fwd_send.at[pair], fwd_recv.at[pair]),
        ):
            copy = pltpu.make_async_remote_copy(
                src_ref=src, dst_ref=dst, send_sem=ssem, recv_sem=rsem, device_id=to_prev, device_id_type=MESH
            )
            if start:
                copy.start()
            else:
                copy.wait_send()

    def store(pair):
        at = pl.ds(pl.multiple_of(pair * 256, 256), 256)
        return pltpu.make_async_copy(dqo.at[:, at, :], dq_hbm.at[:, at, :], store_sem.at[pair])

    @pl.loop(0, 9)
    def _(step):
        @pl.when(step < 8)
        def _():
            pair = source(step)
            for w in range(2):
                sender = pair * 2 + w

                @pl.when(sender != head)
                def _():
                    waiting(dels.at[sender], del_recv.at[sender], {"head": peers[0]})
                    waiting(cots.at[sender], cot_recv.at[sender], {"head": peers[0]})

            @pl.when(pair < 4)
            def _():
                forward(pair, True)

            use_pair(pair, 1280, True)
            store(pair).start()

        @pl.when(step > 0)
        def _():
            pair = source(step - 1)
            for k in range(4):

                @pl.when(pair == k)
                def _():
                    past = pl.ds(16 + k * 2, 2)
                    waiting(dels.at[past], fwd_del_recv.at[k], to_prev)
                    waiting(cots.at[past], fwd_recv.at[k], to_prev)
                    use_pair(8 + k, 1024 - 256 * k, False)

    dko[...] = (dka[pl.ds(1024, 2048), :] * SCALE).astype(BF)
    dvo[...] = dva[pl.ds(1024, 2048), :].astype(BF)
    stores = [
        pltpu.make_async_copy(dko, dk_hbm.at[0], store_sem.at[8]),
        pltpu.make_async_copy(dvo, dv_hbm.at[0], store_sem.at[9]),
    ]
    for copy in stores:
        copy.start()
    for copy in sends:
        copy.wait_send()
    for k in range(4):
        forward(k, False)
    for pair in range(8):
        store(pair).wait()
    for copy in stores:
        copy.wait()


def body(queries, key_states, value_states, attn_output, out_cotangent, logsumexp, doc_start):
    hbm = pl.BlockSpec(memory_space=pl.ANY)
    dma = pltpu.SemaphoreType.DMA
    return pl.pallas_call(
        attention_kernel,
        name="attention_backward",
        out_shape=(
            jax.ShapeDtypeStruct((2, 2048, 128), BF),
            jax.ShapeDtypeStruct((1, 2048, 128), BF),
            jax.ShapeDtypeStruct((1, 2048, 128), BF),
        ),
        in_specs=[hbm] * 7,
        out_specs=(hbm, hbm, hbm),
        scratch_shapes=[
            pltpu.VMEM((2, 3072, 128), BF),
            pltpu.VMEM((3072, 128), BF),
            pltpu.VMEM((3072, 128), BF),
            pltpu.VMEM((128, 3072), BF),
            pltpu.VMEM((128, 4096), BF),
            pltpu.VMEM((128, 4096), BF),
            pltpu.VMEM((2, 3072), F32),
            pltpu.VMEM((24, 128), jnp.int32),
            pltpu.VMEM((24, 128, 256), BF),
            pltpu.VMEM((24, 2, 128), F32),
            pltpu.VMEM((16, 2, 128), F32),
            pltpu.VMEM((12, 1280, 512), F32),
            pltpu.VMEM((3072, 128), F32),
            pltpu.VMEM((3072, 128), F32),
            pltpu.VMEM((2, 2048, 128), BF),
            pltpu.VMEM((2048, 128), BF),
            pltpu.VMEM((2048, 128), BF),
            dma((7,)), dma((5,)), dma((5,)), dma((15,)), dma((16,)), dma((15,)), dma((16,)),
            dma((4,)), dma((4,)), dma((4,)), dma((4,)), dma((10,)),
        ],
        compiler_params=pltpu.CompilerParams(collective_id=0, has_side_effects=True, vmem_limit_bytes=58 << 20),
    )(queries, key_states, value_states, attn_output, out_cotangent, logsumexp, doc_start.reshape(16, 128))


def solution(mesh):
    return jax.shard_map(
        body,
        mesh=mesh,
        in_specs=(
            P("head", "ctx", None),
            P("head", "ctx", None),
            P("head", "ctx", None),
            P(("ctx", "head"), None),
            P(("ctx", "head"), None),
            P("head", "ctx"),
            P("ctx"),
        ),
        out_specs=(P("head", "ctx", None), P("head", "ctx", None), P("head", "ctx", None)),
        check_vma=False,
    )
```

```python
import functools

import jax
import jax.numpy as jnp
from jax import lax
from jax.experimental import pallas as pl
from jax.experimental.pallas import tpu as pltpu
from jax.sharding import PartitionSpec as P

W = 1024
QPRE = 168
SCALE = QPRE ** (-0.5)
LOG2E = 1.4426950408889634
MESH = pl.DeviceIdType.MESH
BF = jnp.bfloat16
LAG = 4
F32 = jnp.float32
NT = (((1,), (1,)), ((), ()))
NN = (((1,), (0,)), ((), ()))
PEERS = ((0, 1), (1, 0), (7, 0), (1, 1), (7, 1), (2, 0), (6, 0), (2, 1), (6, 1), (3, 0), (5, 0), (3, 1), (5, 1), (4, 0), (4, 1))


def mm(a, b, dims):
    return lax.dot_general(a, b, dims, preferred_element_type=F32)


def side(parts, axis):
    return parts[0] if len(parts) == 1 else jnp.concatenate(parts, axis=axis)


def segments(rows):
    if rows > 1152:
        return ((0, 128, "A"), (128, 1024, "AB"), (1152, 128, "B"))
    return ((0, 128, "A"), (128, rows - 128, "AB"))


def attention_kernel(
    q_hbm, k_hbm, v_hbm, out_hbm, cot_hbm, lse_hbm, doc_hbm,
    dqo, dko, dvo,
    qv, kx, vx, kt, outv, cotv, lsev, docv, cots, dels, delsrc, probs, dka, dva,
    load_sem, halo_send, halo_recv, cot_send, cot_recv, del_send, del_recv,
    fwd_send, fwd_recv, fwd_del_send, fwd_del_recv,
):
    ctx = lax.axis_index("ctx")
    head = lax.axis_index("head")
    z, x = head // 2, head % 2
    nxt, prv = lax.rem(ctx + 1, 16), lax.rem(ctx + 15, 16)
    peers = [lax.rem(z + dz, 8) * 2 + lax.rem(x + dx, 2) for dz, dx in PEERS]

    barrier = pltpu.get_barrier_semaphore()
    for peer in peers:
        pl.semaphore_signal(barrier, inc=1, device_id={"head": peer}, device_id_type=MESH)
    for peer in (nxt, prv):
        pl.semaphore_signal(barrier, inc=1, device_id={"ctx": peer}, device_id_type=MESH)

    loads = [
        pltpu.make_async_copy(cot_hbm, cotv, load_sem.at[0]),
        pltpu.make_async_copy(out_hbm, outv, load_sem.at[1]),
        pltpu.make_async_copy(q_hbm, qv.at[:, pl.ds(0, 2048), :], load_sem.at[2]),
        pltpu.make_async_copy(k_hbm.at[0], kx.at[pl.ds(1024, 2048), :], load_sem.at[3]),
        pltpu.make_async_copy(v_hbm.at[0], vx.at[pl.ds(1024, 2048), :], load_sem.at[4]),
        pltpu.make_async_copy(lse_hbm, lsev.at[:, pl.ds(0, 2048)], load_sem.at[5]),
        pltpu.make_async_copy(doc_hbm, docv.at[pl.ds(0, 16), :], load_sem.at[6]),
    ]
    for load in loads:
        load.start()

    loads[0].wait()
    loads[1].wait()
    lane = lax.broadcasted_iota(jnp.int32, (128, 128), 1)
    rows_delta = jnp.zeros((128, 128), F32)
    for h in range(32):
        cols = slice(h * 128, (h + 1) * 128)
        product = cotv[:, cols].astype(F32) * outv[:, cols].astype(F32)
        rows_delta = jnp.where(lane == h, jnp.sum(product, axis=1, keepdims=True), rows_delta)
    rows_delta = rows_delta.T
    for j in range(16):
        delsrc[j] = rows_delta[2 * j : 2 * j + 2]

    pl.semaphore_wait(barrier, 17)
    sends = []
    has_prev, has_next = ctx > 0, ctx < 15

    def remote(src, dst, n, where):
        return pltpu.make_async_remote_copy(
            src_ref=src, dst_ref=dst, send_sem=halo_send.at[n], recv_sem=halo_recv.at[n], device_id=where, device_id_type=MESH
        )

    def halo_to_next():
        last, before = pl.ds(1024, 1024), pl.ds(0, 1024)
        return [
            remote(k_hbm.at[0, last, :], kx.at[before, :], 0, {"ctx": nxt}),
            remote(v_hbm.at[0, last, :], vx.at[before, :], 1, {"ctx": nxt}),
        ]

    def halo_to_prev():
        first, past = pl.ds(0, 1024), pl.ds(2048, 1024)
        return [
            remote(lse_hbm.at[:, first], lsev.at[:, past], 2, {"ctx": prv}),
            remote(doc_hbm.at[pl.ds(0, 8), :], docv.at[pl.ds(16, 8), :], 3, {"ctx": prv}),
            remote(q_hbm.at[:, first, :], qv.at[:, past, :], 4, {"ctx": prv}),
        ]

    def send(src, dst, send_sem, recv_sem, where):
        copy = pltpu.make_async_remote_copy(
            src_ref=src, dst_ref=dst, send_sem=send_sem, recv_sem=recv_sem, device_id=where, device_id_type=MESH
        )
        copy.start()
        return copy

    for n, peer in enumerate(peers):
        sends.append(send(delsrc.at[peer], dels.at[head], del_send.at[n], del_recv.at[head], {"head": peer}))
    for n, peer in enumerate(peers):
        cols = pl.ds(pl.multiple_of(peer * 256, 256), 256)
        sends.append(send(cotv.at[:, cols], cots.at[head], cot_send.at[n], cot_recv.at[head], {"head": peer}))
        if n == 4:

            @pl.when(has_next)
            def _():
                for copy in halo_to_next():
                    copy.start()

            @pl.when(has_prev)
            def _():
                for copy in halo_to_prev():
                    copy.start()

    cots[head] = cotv[:, pl.ds(pl.multiple_of(head * 256, 256), 256)]
    dels[head] = delsrc[head]
    dka[...] = jnp.zeros_like(dka)
    dva[...] = jnp.zeros_like(dva)

    def waiting(dst, recv_sem, where):
        pltpu.make_async_remote_copy(
            src_ref=dst, dst_ref=dst, send_sem=cot_send.at[0], recv_sem=recv_sem, device_id=where, device_id_type=MESH
        ).wait_recv()

    base = ctx * 2048
    col = lax.broadcasted_iota(jnp.int32, (1, 128), 1)

    def queries_of(q0):
        return jnp.concatenate([qv[0, pl.ds(q0, 128), :], qv[1, pl.ds(q0, 128), :]], axis=0)

    def make_probs(pair, rows):
        for which in range(2):
            chunk = pair * 2 + which
            q0 = pl.multiple_of(chunk * 128, 128)
            query = queries_of(q0)
            at = pl.ds(q0, 128)
            lse = jnp.concatenate([lsev[0:1, at], lsev[1:2, at]], axis=1) * LOG2E
            low = jnp.maximum(docv[pl.ds(chunk, 1), :] - base + (W - q0), col + 1)
            low = jnp.concatenate([low, low], axis=1)
            high = jnp.concatenate([col, col], axis=1) + W
            span = min(1152, rows - 128 * which)
            for first, count in ((0, min(span, 1024)), (1024, span - 1024)):
                if count <= 0:
                    continue
                scores = mm(kx[pl.ds(q0 + first, count), :], query, NT)
                row = lax.broadcasted_iota(jnp.int32, (count, 256), 0) + first
                allowed = row >= low
                if first == 1024:
                    allowed = allowed & (row <= high)
                value = jnp.where(allowed, jnp.exp2(scores * (SCALE * LOG2E) - lse), 0.0)
                probs[pair, pl.ds(128 * which + first, count), pl.ds(256 * which, 256)] = value

    def use_pair(pair, rows, with_queries):
        q0 = pl.multiple_of(pair * 256, 256)
        query, cot, delta, grads = [], [], [], [[], []]
        for which in range(2):
            chunk = pair * 2 + which
            query.append(queries_of(q0 + 128 * which))
            block = cots[chunk]
            cot.append(jnp.concatenate([block[:, :128], block[:, 128:]], axis=0))
            both = dels[chunk]
            delta.append(jnp.concatenate([both[0:1], both[1:2]], axis=1))
        for first, count, whom in segments(rows):
            at = pl.ds(q0 + first, count)
            used = [w for w in range(2) if "AB"[w] in whom]
            low_probs, low_scores = [], []
            for w in used:
                prob = probs[pair, pl.ds(first, count), pl.ds(256 * w, 256)]
                dprobs = mm(vx[at, :], cot[w], NT)
                dscores = (prob * (dprobs - delta[w])).astype(BF)
                low_probs.append(prob.astype(BF))
                low_scores.append(dscores)
                if with_queries:
                    grads[w].append(mm(kt[:, at], dscores, NN))
            dva[at, :] += mm(side(low_probs, 1), side([cot[w] for w in used], 0), NN)
            dka[at, :] += mm(side(low_scores, 1), side([query[w] for w in used], 0), NN)
        if with_queries:
            for w in range(2):
                total = functools.reduce(jnp.add, grads[w]).T
                total = (total * SCALE).astype(BF)
                at = pl.ds(q0 + 128 * w, 128)
                dqo[0, at, :] = total[:128]
                dqo[1, at, :] = total[128:]

    for load in loads[2:]:
        load.wait()
    for b in range(8, 24):
        kt[:, b * 128 : (b + 1) * 128] = kx[pl.ds(b * 128, 128), :].T

    @pl.loop(4, 8)
    def _(pair):
        make_probs(pair, 1280)

    to_next, to_prev = {"ctx": nxt}, {"ctx": prv}

    @pl.when(has_prev)
    def _():
        waiting(kx.at[pl.ds(0, 1024), :], halo_recv.at[0], to_next)

    @pl.when(jnp.logical_not(has_prev))
    def _():
        kx[pl.ds(0, 1024), :] = jnp.zeros((1024, 128), BF)
        vx[pl.ds(0, 1024), :] = jnp.zeros((1024, 128), BF)

    for b in range(8):
        kt[:, b * 128 : (b + 1) * 128] = kx[pl.ds(b * 128, 128), :].T

    @pl.loop(0, 4)
    def _(pair):
        make_probs(pair, 1280)

    @pl.when(has_next)
    def _():
        waiting(lsev.at[:, pl.ds(2048, 1024)], halo_recv.at[2], to_prev)
        waiting(docv.at[pl.ds(16, 8), :], halo_recv.at[3], to_prev)
        waiting(qv.at[:, pl.ds(2048, 1024), :], halo_recv.at[4], to_prev)
        for k in range(4):
            make_probs(8 + k, 1024 - 256 * k)

    @pl.when(has_prev)
    def _():
        waiting(vx.at[pl.ds(0, 1024), :], halo_recv.at[1], to_next)

    def source(step):
        far = (step + 1) // 2
        return lax.rem(z + jnp.where(step % 2 == 1, 8 - far, far), 8)

    def forward(pair, start):
        two = pl.ds(pair * 2, 2)
        past = pl.ds(16 + pair * 2, 2)
        for src, dst, ssem, rsem in (
            (dels.at[two], dels.at[past], fwd_del_send.at[pair], fwd_del_recv.at[pair]),
            (cots.at[two], cots.at[past], fwd_send.at[pair], fwd_recv.at[pair]),
        ):
            copy = pltpu.make_async_remote_copy(
                src_ref=src, dst_ref=dst, send_sem=ssem, recv_sem=rsem, device_id=to_prev, device_id_type=MESH
            )
            if start:
                copy.start()
            else:
                copy.wait_send()

    @pl.loop(0, 8 + LAG)
    def _(step):
        @pl.when(step < 8)
        def _():
            pair = source(step)
            for w in range(2):
                sender = pair * 2 + w

                @pl.when(sender != head)
                def _():
                    waiting(dels.at[sender], del_recv.at[sender], {"head": peers[0]})
                    waiting(cots.at[sender], cot_recv.at[sender], {"head": peers[0]})

            @pl.when(has_prev & (pair < 4))
            def _():
                forward(pair, True)

            use_pair(pair, 1280, True)

        @pl.when(has_next & (step >= LAG))
        def _():
            pair = source(step - LAG)
            for k in range(4):

                @pl.when(pair == k)
                def _():
                    past = pl.ds(16 + k * 2, 2)
                    waiting(dels.at[past], fwd_del_recv.at[k], to_prev)
                    waiting(cots.at[past], fwd_recv.at[k], to_prev)
                    use_pair(8 + k, 1024 - 256 * k, False)

    dko[...] = (dka[pl.ds(1024, 2048), :] * SCALE).astype(BF)
    dvo[...] = dva[pl.ds(1024, 2048), :].astype(BF)
    for copy in sends:
        copy.wait_send()

    @pl.when(has_next)
    def _():
        for copy in halo_to_next():
            copy.wait_send()

    @pl.when(has_prev)
    def _():
        for copy in halo_to_prev():
            copy.wait_send()
        for k in range(4):
            forward(k, False)


def write_kernel(dq, dk, dv, dq_hbm, dk_hbm, dv_hbm, sem):
    copies = [
        pltpu.make_async_copy(src, dst, sem.at[n])
        for n, (src, dst) in enumerate(((dq, dq_hbm), (dk, dk_hbm.at[0]), (dv, dv_hbm.at[0])))
    ]
    for copy in copies:
        copy.start()
    for copy in copies:
        copy.wait()


def body(queries, key_states, value_states, attn_output, out_cotangent, logsumexp, doc_start):
    hbm = pl.BlockSpec(memory_space=pl.ANY)
    dma = pltpu.SemaphoreType.DMA
    vmem = pl.BlockSpec(memory_space=pltpu.VMEM)
    grads = pl.pallas_call(
        attention_kernel,
        name="attention_backward",
        out_shape=(pltpu.VMEM((2, 2048, 128), BF), pltpu.VMEM((2048, 128), BF), pltpu.VMEM((2048, 128), BF)),
        in_specs=[hbm] * 7,
        out_specs=(vmem, vmem, vmem),
        scratch_shapes=[
            pltpu.VMEM((2, 3072, 128), BF),
            pltpu.VMEM((3072, 128), BF),
            pltpu.VMEM((3072, 128), BF),
            pltpu.VMEM((128, 3072), BF),
            pltpu.VMEM((128, 4096), BF),
            pltpu.VMEM((128, 4096), BF),
            pltpu.VMEM((2, 3072), F32),
            pltpu.VMEM((24, 128), jnp.int32),
            pltpu.VMEM((24, 128, 256), BF),
            pltpu.VMEM((24, 2, 128), F32),
            pltpu.VMEM((16, 2, 128), F32),
            pltpu.VMEM((12, 1280, 512), F32),
            pltpu.VMEM((3072, 128), F32),
            pltpu.VMEM((3072, 128), F32),
            dma((7,)), dma((5,)), dma((5,)), dma((15,)), dma((16,)), dma((15,)), dma((16,)),
            dma((4,)), dma((4,)), dma((4,)), dma((4,)),
        ],
        compiler_params=pltpu.CompilerParams(collective_id=0, has_side_effects=True, vmem_limit_bytes=56 << 20),
    )(queries, key_states, value_states, attn_output, out_cotangent, logsumexp, doc_start.reshape(16, 128))
    return pl.pallas_call(
        write_kernel,
        name="write_gradients",
        out_shape=(
            jax.ShapeDtypeStruct((2, 2048, 128), BF),
            jax.ShapeDtypeStruct((1, 2048, 128), BF),
            jax.ShapeDtypeStruct((1, 2048, 128), BF),
        ),
        in_specs=[vmem] * 3,
        out_specs=(hbm, hbm, hbm),
        scratch_shapes=[dma((3,))],
    )(*[pltpu.with_memory_space_constraint(grad, pltpu.VMEM) for grad in grads])


def solution(mesh):
    return jax.shard_map(
        body,
        mesh=mesh,
        in_specs=(
            P("head", "ctx", None),
            P("head", "ctx", None),
            P("head", "ctx", None),
            P(("ctx", "head"), None),
            P(("ctx", "head"), None),
            P("head", "ctx"),
            P("ctx"),
        ),
        out_specs=(P("head", "ctx", None), P("head", "ctx", None), P("head", "ctx", None)),
        check_vma=False,
    )
```

```python
import jax
import jax.numpy as jnp
from jax import lax
from jax.experimental import pallas as pl
from jax.experimental.pallas import tpu as pltpu
from jax.sharding import PartitionSpec as P

W = 1024
QPRE = 168
SCALE = QPRE ** (-0.5)
LOG2E = 1.4426950408889634
MESH = pl.DeviceIdType.MESH
BF = jnp.bfloat16
LAG = 8
PRE = 2
F32 = jnp.float32
NT = (((1,), (1,)), ((), ()))
NN = (((1,), (0,)), ((), ()))
PEERS = ((0, 0), (1, 0), (7, 0), (2, 0), (6, 0), (3, 0), (5, 0), (4, 0), (0, 1), (1, 1), (7, 1), (2, 1), (6, 1), (3, 1), (5, 1), (4, 1))


def mm(a, b, dims):
    return lax.dot_general(a, b, dims, preferred_element_type=F32)


def attention_kernel(
    q_hbm, k_hbm, v_hbm, out_hbm, cot_hbm, lse_hbm, doc_hbm,
    dqo, dko, dvo,
    qv, kx, vx, kt, outv, cotv, lsev, docv, cots, dels, delsrc, probs, dka, dva,
    load_sem, halo_send, halo_recv, cot_send, cot_recv, del_send, del_recv,
    fwd_send, fwd_recv,
):
    ctx = lax.axis_index("ctx")
    head = lax.axis_index("head")
    z, x = head // 2, head % 2
    nxt, prv = lax.rem(ctx + 1, 16), lax.rem(ctx + 15, 16)
    peers = [lax.rem(z + dz, 8) * 2 + lax.rem(x + dx, 2) for dz, dx in PEERS[1:]]

    barrier = pltpu.get_barrier_semaphore()
    for peer in peers:
        pl.semaphore_signal(barrier, inc=1, device_id={"head": peer}, device_id_type=MESH)
    for peer in (nxt, prv):
        pl.semaphore_signal(barrier, inc=1, device_id={"ctx": peer}, device_id_type=MESH)

    loads = [
        pltpu.make_async_copy(cot_hbm, cotv, load_sem.at[0]),
        pltpu.make_async_copy(out_hbm, outv, load_sem.at[1]),
        pltpu.make_async_copy(q_hbm, qv.at[:, pl.ds(0, 2048), :], load_sem.at[2]),
        pltpu.make_async_copy(k_hbm.at[0], kx.at[pl.ds(1024, 2048), :], load_sem.at[3]),
        pltpu.make_async_copy(v_hbm.at[0], vx.at[pl.ds(1024, 2048), :], load_sem.at[4]),
        pltpu.make_async_copy(lse_hbm, lsev.at[:, pl.ds(0, 2048)], load_sem.at[5]),
        pltpu.make_async_copy(doc_hbm, docv.at[pl.ds(0, 16), :], load_sem.at[6]),
    ]
    for load in loads:
        load.start()

    pl.semaphore_wait(barrier, 17)
    sends = []
    has_prev, has_next = ctx > 0, ctx < 15

    def remote(src, dst, n, where):
        return pltpu.make_async_remote_copy(
            src_ref=src, dst_ref=dst, send_sem=halo_send.at[n], recv_sem=halo_recv.at[n], device_id=where, device_id_type=MESH
        )

    def halo_to_next():
        last, before = pl.ds(1024, 1024), pl.ds(0, 1024)
        return [
            remote(k_hbm.at[0, last, :], kx.at[before, :], 0, {"ctx": nxt}),
            remote(v_hbm.at[0, last, :], vx.at[before, :], 1, {"ctx": nxt}),
        ]

    def halo_to_prev():
        first, past = pl.ds(0, 1024), pl.ds(2048, 1024)
        return [
            remote(lse_hbm.at[:, first], lsev.at[:, past], 2, {"ctx": prv}),
            remote(doc_hbm.at[pl.ds(0, 8), :], docv.at[pl.ds(16, 8), :], 3, {"ctx": prv}),
            remote(q_hbm.at[:, first, :], qv.at[:, past, :], 4, {"ctx": prv}),
        ]

    def send_past():
        @pl.when(has_prev)
        def _():
            for copy in halo_to_prev():
                copy.start()

    def send(src, dst, send_sem, recv_sem, where):
        copy = pltpu.make_async_remote_copy(
            src_ref=src, dst_ref=dst, send_sem=send_sem, recv_sem=recv_sem, device_id=where, device_id_type=MESH
        )
        copy.start()
        return copy

    def pick(step, values):
        picked = jnp.int32(0)
        for n, value in enumerate(values):
            picked = jnp.where(step == n, value, picked)
        return picked

    def block_copy(n):
        dz, dx = PEERS[n]
        peer = lax.rem(z + dz, 8) * 2 + lax.rem(x + dx, 2)
        return pltpu.make_async_remote_copy(
            src_ref=cot_hbm.at[:, pl.ds(pl.multiple_of(peer * 256, 256), 256)],
            dst_ref=cots.at[head],
            send_sem=cot_send.at[n - 1],
            recv_sem=cot_recv.at[head],
            device_id={"head": peer},
            device_id_type=MESH,
        )

    @pl.when(has_next)
    def _():
        for copy in halo_to_next():
            copy.start()

    for n in range(1, PRE + 1):
        block_copy(n).start()

    loads[0].wait()
    loads[1].wait()
    lane = lax.broadcasted_iota(jnp.int32, (128, 128), 1)
    rows_delta = jnp.zeros((128, 128), F32)
    for h in range(32):
        cols = slice(h * 128, (h + 1) * 128)
        product = cotv[:, cols].astype(F32) * outv[:, cols].astype(F32)
        rows_delta = jnp.where(lane == h, jnp.sum(product, axis=1, keepdims=True), rows_delta)
    rows_delta = rows_delta.T
    for j in range(16):
        delsrc[j] = rows_delta[2 * j : 2 * j + 2]

    for n, peer in enumerate(peers):
        sends.append(send(delsrc.at[peer], dels.at[head], del_send.at[n], del_recv.at[head], {"head": peer}))
    for n in range(PRE + 1, 16):
        block_copy(n).start()
    send_past()

    cots[head] = cotv[:, pl.ds(pl.multiple_of(head * 256, 256), 256)]
    dels[head] = delsrc[head]
    kx[pl.ds(3072, 128), :] = jnp.zeros((128, 128), BF)
    vx[pl.ds(3072, 128), :] = jnp.zeros((128, 128), BF)
    dka[...] = jnp.zeros_like(dka)
    dva[...] = jnp.zeros_like(dva)

    def waiting(dst, recv_sem, where):
        pltpu.make_async_remote_copy(
            src_ref=dst, dst_ref=dst, send_sem=cot_send.at[0], recv_sem=recv_sem, device_id=where, device_id_type=MESH
        ).wait_recv()

    base = ctx * 2048
    col = lax.broadcasted_iota(jnp.int32, (1, 128), 1)

    def queries_of(q0):
        return jnp.concatenate([qv[0, pl.ds(q0, 128), :], qv[1, pl.ds(q0, 128), :]], axis=0)

    def make_probs(chunk, span, keep):
        q0 = pl.multiple_of(chunk * 128, 128)
        query = queries_of(q0)
        at = pl.ds(q0, 128)
        lse = jnp.concatenate([lsev[0:1, at], lsev[1:2, at]], axis=1) * LOG2E
        low = jnp.maximum(docv[pl.ds(chunk, 1), :] - base + (W - q0), col + 1)
        low = jnp.concatenate([low, low], axis=1)
        high = jnp.concatenate([col, col], axis=1) + W
        for first, count in ((0, min(span, 1024)), (1024, span - 1024)):
            if count <= 0:
                continue
            scores = mm(kx[pl.ds(q0 + first, count), :], query, NT)
            row = lax.broadcasted_iota(jnp.int32, (count, 256), 0) + first
            allowed = row >= low
            if first == 1024:
                allowed = allowed & (row <= high)
            keep(first, count, jnp.where(allowed, jnp.exp2(scores * (SCALE * LOG2E) - lse), 0.0))

    def chunk_probs(chunk):
        def keep(first, count, value):
            probs[chunk, pl.ds(first, count), :] = value

        make_probs(chunk, 1152, keep)

    def cotangents_of(chunk):
        block = cots[chunk]
        return jnp.concatenate([block[:, :128], block[:, 128:]], axis=0)

    def delta_of(chunk):
        both = dels[chunk]
        return jnp.concatenate([both[0:1], both[1:2]], axis=1)

    def use_chunk(chunk):
        q0 = pl.multiple_of(chunk * 128, 128)
        query, cot, delta = queries_of(q0), cotangents_of(chunk), delta_of(chunk)
        at = pl.ds(q0, 1152)
        prob = probs[chunk]
        dscores = (prob * (mm(vx[at, :], cot, NT) - delta)).astype(BF)
        dva[at, :] += mm(prob.astype(BF), cot, NN)
        dka[at, :] += mm(dscores, query, NN)
        grad = (mm(kt[:, at], dscores, NN).T * SCALE).astype(BF)
        dqo[0, pl.ds(q0, 128), :] = grad[:128]
        dqo[1, pl.ds(q0, 128), :] = grad[128:]

    def use_past_chunk(chunk, rows):
        q0 = pl.multiple_of(2048 + chunk * 128, 128)
        query, cot, delta = queries_of(q0), cotangents_of(16 + chunk), delta_of(16 + chunk)
        at = pl.ds(q0, rows)

        def keep(first, count, prob):
            dscores = (prob * (mm(vx[at, :], cot, NT) - delta)).astype(BF)
            dva[at, :] += mm(prob.astype(BF), cot, NN)
            dka[at, :] += mm(dscores, query, NN)

        make_probs(16 + chunk, rows, keep)

    for load in loads[2:]:
        load.wait()
    for b in range(8, 24):
        kt[:, b * 128 : (b + 1) * 128] = kx[pl.ds(b * 128, 128), :].T

    @pl.loop(8, 16, unroll=2)
    def _(chunk):
        chunk_probs(chunk)

    to_next, to_prev = {"ctx": nxt}, {"ctx": prv}

    @pl.when(has_prev)
    def _():
        waiting(kx.at[pl.ds(0, 1024), :], halo_recv.at[0], to_next)

    @pl.when(jnp.logical_not(has_prev))
    def _():
        kx[pl.ds(0, 1024), :] = jnp.zeros((1024, 128), BF)
        vx[pl.ds(0, 1024), :] = jnp.zeros((1024, 128), BF)

    for b in range(8):
        kt[:, b * 128 : (b + 1) * 128] = kx[pl.ds(b * 128, 128), :].T

    @pl.loop(0, 8, unroll=2)
    def _(chunk):
        chunk_probs(chunk)

    @pl.when(has_prev)
    def _():
        waiting(vx.at[pl.ds(0, 1024), :], halo_recv.at[1], to_next)

    def source(step):
        back, across = pick(step, [8 - p[0] for p in PEERS]), pick(step, [p[1] for p in PEERS])
        return lax.rem(z + back, 8) * 2 + lax.rem(x + across, 2)

    def forward(chunk):
        return [
            pltpu.make_async_remote_copy(
                src_ref=ref.at[chunk],
                dst_ref=ref.at[16 + chunk],
                send_sem=fwd_send.at[n, chunk],
                recv_sem=fwd_recv.at[n, chunk],
                device_id=to_prev,
                device_id_type=MESH,
            )
            for n, ref in enumerate((dels, cots))
        ]

    @pl.loop(0, 16 + LAG)
    def _(step):
        @pl.when(step < 16)
        def _():
            chunk = source(step)

            @pl.when(chunk != head)
            def _():
                waiting(dels.at[chunk], del_recv.at[chunk], {"head": peers[0]})
                waiting(cots.at[chunk], cot_recv.at[chunk], {"head": peers[0]})

            @pl.when(has_prev & (chunk < 8))
            def _():
                for copy in forward(chunk):
                    copy.start()

            use_chunk(chunk)

        @pl.when(has_next & (step == LAG))
        def _():
            waiting(lsev.at[:, pl.ds(2048, 1024)], halo_recv.at[2], to_prev)
            waiting(docv.at[pl.ds(16, 8), :], halo_recv.at[3], to_prev)
            waiting(qv.at[:, pl.ds(2048, 1024), :], halo_recv.at[4], to_prev)

        @pl.when(has_next & (step >= LAG))
        def _():
            chunk = source(step - LAG)

            @pl.when(chunk < 8)
            def _():
                waiting(dels.at[16 + chunk], fwd_recv.at[0, chunk], to_prev)
                waiting(cots.at[16 + chunk], fwd_recv.at[1, chunk], to_prev)

            for k in range(4):

                @pl.when(chunk // 2 == k)
                def _():
                    use_past_chunk(chunk, 1024 - 256 * k)

    dko[...] = (dka[pl.ds(1024, 2048), :] * SCALE).astype(BF)
    dvo[...] = dva[pl.ds(1024, 2048), :].astype(BF)
    for copy in sends:
        copy.wait_send()
    for n in range(1, 16):
        block_copy(n).wait_send()

    @pl.when(has_next)
    def _():
        for copy in halo_to_next():
            copy.wait_send()

    @pl.when(has_prev)
    def _():
        for copy in halo_to_prev():
            copy.wait_send()
        for chunk in range(8):
            for copy in forward(chunk):
                copy.wait_send()


def write_kernel(dq, dk, dv, dq_hbm, dk_hbm, dv_hbm, sem):
    copies = [
        pltpu.make_async_copy(src, dst, sem.at[n])
        for n, (src, dst) in enumerate(((dq, dq_hbm), (dk, dk_hbm.at[0]), (dv, dv_hbm.at[0])))
    ]
    for copy in copies:
        copy.start()
    for copy in copies:
        copy.wait()


def body(queries, key_states, value_states, attn_output, out_cotangent, logsumexp, doc_start):
    hbm = pl.BlockSpec(memory_space=pl.ANY)
    dma = pltpu.SemaphoreType.DMA
    vmem = pl.BlockSpec(memory_space=pltpu.VMEM)
    grads = pl.pallas_call(
        attention_kernel,
        name="attention_backward",
        out_shape=(pltpu.VMEM((2, 2048, 128), BF), pltpu.VMEM((2048, 128), BF), pltpu.VMEM((2048, 128), BF)),
        in_specs=[hbm] * 7,
        out_specs=(vmem, vmem, vmem),
        scratch_shapes=[
            pltpu.VMEM((2, 3072, 128), BF),
            pltpu.VMEM((3200, 128), BF),
            pltpu.VMEM((3200, 128), BF),
            pltpu.VMEM((128, 3072), BF),
            pltpu.VMEM((128, 4096), BF),
            pltpu.VMEM((128, 4096), BF),
            pltpu.VMEM((2, 3072), F32),
            pltpu.VMEM((24, 128), jnp.int32),
            pltpu.VMEM((24, 128, 256), BF),
            pltpu.VMEM((24, 2, 128), F32),
            pltpu.VMEM((16, 2, 128), F32),
            pltpu.VMEM((16, 1152, 256), F32),
            pltpu.VMEM((3200, 128), F32),
            pltpu.VMEM((3200, 128), F32),
            dma((7,)), dma((5,)), dma((5,)), dma((15,)), dma((16,)), dma((15,)), dma((16,)),
            dma((2, 8)), dma((2, 8)),
        ],
        compiler_params=pltpu.CompilerParams(collective_id=0, has_side_effects=True, vmem_limit_bytes=56 << 20),
    )(queries, key_states, value_states, attn_output, out_cotangent, logsumexp, doc_start.reshape(16, 128))
    return pl.pallas_call(
        write_kernel,
        name="write_gradients",
        out_shape=(
            jax.ShapeDtypeStruct((2, 2048, 128), BF),
            jax.ShapeDtypeStruct((1, 2048, 128), BF),
            jax.ShapeDtypeStruct((1, 2048, 128), BF),
        ),
        in_specs=[vmem] * 3,
        out_specs=(hbm, hbm, hbm),
        scratch_shapes=[dma((3,))],
    )(*[pltpu.with_memory_space_constraint(grad, pltpu.VMEM) for grad in grads])


def solution(mesh):
    return jax.shard_map(
        body,
        mesh=mesh,
        in_specs=(
            P("head", "ctx", None),
            P("head", "ctx", None),
            P("head", "ctx", None),
            P(("ctx", "head"), None),
            P(("ctx", "head"), None),
            P("head", "ctx"),
            P("ctx"),
        ),
        out_specs=(P("head", "ctx", None), P("head", "ctx", None), P("head", "ctx", None)),
        check_vma=False,
    )
```

```python
import jax
import jax.numpy as jnp
from jax import lax
from jax.experimental import pallas as pl
from jax.experimental.pallas import tpu as pltpu
from jax.sharding import PartitionSpec as P

W = 1024
QPRE = 168
SCALE = QPRE ** (-0.5)
LOG2E = 1.4426950408889634
MESH = pl.DeviceIdType.MESH
BF = jnp.bfloat16
LAG = 8
PAST_AT = 3
PRE = 2
F32 = jnp.float32
NT = (((1,), (1,)), ((), ()))
NN = (((1,), (0,)), ((), ()))
PEERS = ((0, 0), (1, 0), (7, 0), (2, 0), (6, 0), (3, 0), (5, 0), (4, 0), (0, 1), (1, 1), (7, 1), (2, 1), (6, 1), (3, 1), (5, 1), (4, 1))


def mm(a, b, dims):
    return lax.dot_general(a, b, dims, preferred_element_type=F32)


def attention_kernel(
    q_hbm, k_hbm, v_hbm, out_hbm, cot_hbm, lse_hbm, doc_hbm,
    dqo, dko, dvo,
    qv, kx, vx, kt, outv, cotv, lsev, docv, cots, dels, delsrc, probs, past_probs, dka, dva,
    load_sem, halo_send, halo_recv, cot_send, cot_recv, del_send, del_recv,
    fwd_send, fwd_recv,
):
    ctx = lax.axis_index("ctx")
    head = lax.axis_index("head")
    z, x = head // 2, head % 2
    nxt, prv = lax.rem(ctx + 1, 16), lax.rem(ctx + 15, 16)
    peers = [lax.rem(z + dz, 8) * 2 + lax.rem(x + dx, 2) for dz, dx in PEERS[1:]]

    barrier = pltpu.get_barrier_semaphore()
    for peer in peers:
        pl.semaphore_signal(barrier, inc=1, device_id={"head": peer}, device_id_type=MESH)
    for peer in (nxt, prv):
        pl.semaphore_signal(barrier, inc=1, device_id={"ctx": peer}, device_id_type=MESH)

    loads = [
        pltpu.make_async_copy(cot_hbm, cotv, load_sem.at[0]),
        pltpu.make_async_copy(out_hbm, outv, load_sem.at[1]),
        pltpu.make_async_copy(q_hbm, qv.at[:, pl.ds(0, 2048), :], load_sem.at[2]),
        pltpu.make_async_copy(k_hbm.at[0], kx.at[pl.ds(1024, 2048), :], load_sem.at[3]),
        pltpu.make_async_copy(v_hbm.at[0], vx.at[pl.ds(1024, 2048), :], load_sem.at[4]),
        pltpu.make_async_copy(lse_hbm, lsev.at[:, pl.ds(0, 2048)], load_sem.at[5]),
        pltpu.make_async_copy(doc_hbm, docv.at[pl.ds(0, 16), :], load_sem.at[6]),
    ]
    for load in loads:
        load.start()

    pl.semaphore_wait(barrier, 17)
    sends = []
    has_prev, has_next = ctx > 0, ctx < 15

    def remote(src, dst, n, where):
        return pltpu.make_async_remote_copy(
            src_ref=src, dst_ref=dst, send_sem=halo_send.at[n], recv_sem=halo_recv.at[n], device_id=where, device_id_type=MESH
        )

    def halo_to_next():
        last, before = pl.ds(1024, 1024), pl.ds(0, 1024)
        return [
            remote(k_hbm.at[0, last, :], kx.at[before, :], 0, {"ctx": nxt}),
            remote(v_hbm.at[0, last, :], vx.at[before, :], 1, {"ctx": nxt}),
        ]

    def halo_to_prev():
        first, past = pl.ds(0, 1024), pl.ds(2048, 1024)
        return [
            remote(lse_hbm.at[:, first], lsev.at[:, past], 2, {"ctx": prv}),
            remote(doc_hbm.at[pl.ds(0, 8), :], docv.at[pl.ds(16, 8), :], 3, {"ctx": prv}),
            remote(q_hbm.at[:, first, :], qv.at[:, past, :], 4, {"ctx": prv}),
        ]

    def send_past():
        @pl.when(has_prev)
        def _():
            for copy in halo_to_prev():
                copy.start()

    def send(src, dst, send_sem, recv_sem, where):
        copy = pltpu.make_async_remote_copy(
            src_ref=src, dst_ref=dst, send_sem=send_sem, recv_sem=recv_sem, device_id=where, device_id_type=MESH
        )
        copy.start()
        return copy

    def pick(step, values):
        picked = jnp.int32(0)
        for n, value in enumerate(values):
            picked = jnp.where(step == n, value, picked)
        return picked

    def block_copy(n):
        dz, dx = PEERS[n]
        peer = lax.rem(z + dz, 8) * 2 + lax.rem(x + dx, 2)
        return pltpu.make_async_remote_copy(
            src_ref=cot_hbm.at[:, pl.ds(pl.multiple_of(peer * 256, 256), 256)],
            dst_ref=cots.at[head],
            send_sem=cot_send.at[n - 1],
            recv_sem=cot_recv.at[head],
            device_id={"head": peer},
            device_id_type=MESH,
        )

    @pl.when(has_next)
    def _():
        for copy in halo_to_next():
            copy.start()

    for n in range(1, PRE + 1):
        block_copy(n).start()

    loads[0].wait()
    loads[1].wait()
    lane = lax.broadcasted_iota(jnp.int32, (128, 128), 1)
    rows_delta = jnp.zeros((128, 128), F32)
    for h in range(32):
        cols = slice(h * 128, (h + 1) * 128)
        product = cotv[:, cols].astype(F32) * outv[:, cols].astype(F32)
        rows_delta = jnp.where(lane == h, jnp.sum(product, axis=1, keepdims=True), rows_delta)
    rows_delta = rows_delta.T
    for j in range(16):
        delsrc[j] = rows_delta[2 * j : 2 * j + 2]

    for n, peer in enumerate(peers):
        sends.append(send(delsrc.at[peer], dels.at[head], del_send.at[n], del_recv.at[head], {"head": peer}))
    for n in range(PRE + 1, 16):
        block_copy(n).start()
    send_past()

    cots[head] = cotv[:, pl.ds(pl.multiple_of(head * 256, 256), 256)]
    dels[head] = delsrc[head]
    kx[pl.ds(3072, 128), :] = jnp.zeros((128, 128), BF)
    vx[pl.ds(3072, 128), :] = jnp.zeros((128, 128), BF)
    dka[...] = jnp.zeros_like(dka)
    dva[...] = jnp.zeros_like(dva)

    def waiting(dst, recv_sem, where):
        pltpu.make_async_remote_copy(
            src_ref=dst, dst_ref=dst, send_sem=cot_send.at[0], recv_sem=recv_sem, device_id=where, device_id_type=MESH
        ).wait_recv()

    base = ctx * 2048
    col = lax.broadcasted_iota(jnp.int32, (1, 128), 1)

    def queries_of(q0):
        return jnp.concatenate([qv[0, pl.ds(q0, 128), :], qv[1, pl.ds(q0, 128), :]], axis=0)

    def make_probs(chunk, span, keep):
        q0 = pl.multiple_of(chunk * 128, 128)
        query = queries_of(q0)
        at = pl.ds(q0, 128)
        lse = jnp.concatenate([lsev[0:1, at], lsev[1:2, at]], axis=1) * LOG2E
        low = jnp.maximum(docv[pl.ds(chunk, 1), :] - base + (W - q0), col + 1)
        low = jnp.concatenate([low, low], axis=1)
        high = jnp.concatenate([col, col], axis=1) + W
        for first, count in ((0, min(span, 1024)), (1024, span - 1024)):
            if count <= 0:
                continue
            scores = mm(kx[pl.ds(q0 + first, count), :], query, NT)
            row = lax.broadcasted_iota(jnp.int32, (count, 256), 0) + first
            allowed = row >= low
            if first == 1024:
                allowed = allowed & (row <= high)
            keep(first, count, jnp.where(allowed, jnp.exp2(scores * (SCALE * LOG2E) - lse), 0.0))

    def chunk_probs(chunk):
        def keep(first, count, value):
            probs[chunk, pl.ds(first, count), :] = value

        make_probs(chunk, 1152, keep)

    def cotangents_of(chunk):
        block = cots[chunk]
        return jnp.concatenate([block[:, :128], block[:, 128:]], axis=0)

    def delta_of(chunk):
        both = dels[chunk]
        return jnp.concatenate([both[0:1], both[1:2]], axis=1)

    def use_chunk(chunk):
        q0 = pl.multiple_of(chunk * 128, 128)
        query, cot, delta = queries_of(q0), cotangents_of(chunk), delta_of(chunk)
        at = pl.ds(q0, 1152)
        prob = probs[chunk]
        dscores = (prob * (mm(vx[at, :], cot, NT) - delta)).astype(BF)
        dva[at, :] += mm(prob.astype(BF), cot, NN)
        dka[at, :] += mm(dscores, query, NN)
        grad = (mm(kt[:, at], dscores, NN).T * SCALE).astype(BF)
        dqo[0, pl.ds(q0, 128), :] = grad[:128]
        dqo[1, pl.ds(q0, 128), :] = grad[128:]

    def use_past_chunk(chunk, rows):
        q0 = pl.multiple_of(2048 + chunk * 128, 128)
        query, cot, delta = queries_of(q0), cotangents_of(16 + chunk), delta_of(16 + chunk)
        at = pl.ds(q0, rows)

        prob = past_probs[chunk, pl.ds(0, rows), :]
        dscores = (prob * (mm(vx[at, :], cot, NT) - delta)).astype(BF)
        dva[at, :] += mm(prob.astype(BF), cot, NN)
        dka[at, :] += mm(dscores, query, NN)

    def past_chunk_probs(chunk):
        def keep(first, count, value):
            past_probs[chunk, pl.ds(first, count), :] = value

        make_probs(16 + chunk, 1024 - 256 * (chunk // 2), keep)

    for load in loads[2:]:
        load.wait()
    for b in range(8, 24):
        kt[:, b * 128 : (b + 1) * 128] = kx[pl.ds(b * 128, 128), :].T

    @pl.loop(8, 16, unroll=2)
    def _(chunk):
        chunk_probs(chunk)

    to_next, to_prev = {"ctx": nxt}, {"ctx": prv}

    @pl.when(has_prev)
    def _():
        waiting(kx.at[pl.ds(0, 1024), :], halo_recv.at[0], to_next)

    @pl.when(jnp.logical_not(has_prev))
    def _():
        kx[pl.ds(0, 1024), :] = jnp.zeros((1024, 128), BF)
        vx[pl.ds(0, 1024), :] = jnp.zeros((1024, 128), BF)

    for b in range(8):
        kt[:, b * 128 : (b + 1) * 128] = kx[pl.ds(b * 128, 128), :].T

    @pl.loop(0, 8, unroll=2)
    def _(chunk):
        chunk_probs(chunk)

    @pl.when(has_prev)
    def _():
        waiting(vx.at[pl.ds(0, 1024), :], halo_recv.at[1], to_next)

    def source(step):
        back, across = pick(step, [8 - p[0] for p in PEERS]), pick(step, [p[1] for p in PEERS])
        return lax.rem(z + back, 8) * 2 + lax.rem(x + across, 2)

    def forward(chunk):
        return [
            pltpu.make_async_remote_copy(
                src_ref=ref.at[chunk],
                dst_ref=ref.at[16 + chunk],
                send_sem=fwd_send.at[n, chunk],
                recv_sem=fwd_recv.at[n, chunk],
                device_id=to_prev,
                device_id_type=MESH,
            )
            for n, ref in enumerate((dels, cots))
        ]

    @pl.loop(0, 16 + LAG)
    def _(step):
        @pl.when(step < 16)
        def _():
            chunk = source(step)

            @pl.when(chunk != head)
            def _():
                waiting(dels.at[chunk], del_recv.at[chunk], {"head": peers[0]})
                waiting(cots.at[chunk], cot_recv.at[chunk], {"head": peers[0]})

            @pl.when(has_prev & (chunk < 8))
            def _():
                for copy in forward(chunk):
                    copy.start()

            use_chunk(chunk)

        @pl.when(has_next & (step == PAST_AT))
        def _():
            waiting(lsev.at[:, pl.ds(2048, 1024)], halo_recv.at[2], to_prev)
            waiting(docv.at[pl.ds(16, 8), :], halo_recv.at[3], to_prev)
            waiting(qv.at[:, pl.ds(2048, 1024), :], halo_recv.at[4], to_prev)
            for chunk in range(8):
                past_chunk_probs(chunk)

        @pl.when(has_next & (step >= LAG))
        def _():
            chunk = source(step - LAG)

            @pl.when(chunk < 8)
            def _():
                waiting(dels.at[16 + chunk], fwd_recv.at[0, chunk], to_prev)
                waiting(cots.at[16 + chunk], fwd_recv.at[1, chunk], to_prev)

            for k in range(4):

                @pl.when(chunk // 2 == k)
                def _():
                    use_past_chunk(chunk, 1024 - 256 * k)

    dko[...] = (dka[pl.ds(1024, 2048), :] * SCALE).astype(BF)
    dvo[...] = dva[pl.ds(1024, 2048), :].astype(BF)
    for copy in sends:
        copy.wait_send()
    for n in range(1, 16):
        block_copy(n).wait_send()

    @pl.when(has_next)
    def _():
        for copy in halo_to_next():
            copy.wait_send()

    @pl.when(has_prev)
    def _():
        for copy in halo_to_prev():
            copy.wait_send()
        for chunk in range(8):
            for copy in forward(chunk):
                copy.wait_send()


def write_kernel(dq, dk, dv, dq_hbm, dk_hbm, dv_hbm, sem):
    copies = [
        pltpu.make_async_copy(src, dst, sem.at[n])
        for n, (src, dst) in enumerate(((dq, dq_hbm), (dk, dk_hbm.at[0]), (dv, dv_hbm.at[0])))
    ]
    for copy in copies:
        copy.start()
    for copy in copies:
        copy.wait()


def body(queries, key_states, value_states, attn_output, out_cotangent, logsumexp, doc_start):
    hbm = pl.BlockSpec(memory_space=pl.ANY)
    dma = pltpu.SemaphoreType.DMA
    vmem = pl.BlockSpec(memory_space=pltpu.VMEM)
    grads = pl.pallas_call(
        attention_kernel,
        name="attention_backward",
        out_shape=(pltpu.VMEM((2, 2048, 128), BF), pltpu.VMEM((2048, 128), BF), pltpu.VMEM((2048, 128), BF)),
        in_specs=[hbm] * 7,
        out_specs=(vmem, vmem, vmem),
        scratch_shapes=[
            pltpu.VMEM((2, 3072, 128), BF),
            pltpu.VMEM((3200, 128), BF),
            pltpu.VMEM((3200, 128), BF),
            pltpu.VMEM((128, 3072), BF),
            pltpu.VMEM((128, 4096), BF),
            pltpu.VMEM((128, 4096), BF),
            pltpu.VMEM((2, 3072), F32),
            pltpu.VMEM((24, 128), jnp.int32),
            pltpu.VMEM((24, 128, 256), BF),
            pltpu.VMEM((24, 2, 128), F32),
            pltpu.VMEM((16, 2, 128), F32),
            pltpu.VMEM((16, 1152, 256), F32),
            pltpu.VMEM((8, 1024, 256), F32),
            pltpu.VMEM((3200, 128), F32),
            pltpu.VMEM((3200, 128), F32),
            dma((7,)), dma((5,)), dma((5,)), dma((15,)), dma((16,)), dma((15,)), dma((16,)),
            dma((2, 8)), dma((2, 8)),
        ],
        compiler_params=pltpu.CompilerParams(collective_id=0, has_side_effects=True, vmem_limit_bytes=56 << 20),
    )(queries, key_states, value_states, attn_output, out_cotangent, logsumexp, doc_start.reshape(16, 128))
    return pl.pallas_call(
        write_kernel,
        name="write_gradients",
        out_shape=(
            jax.ShapeDtypeStruct((2, 2048, 128), BF),
            jax.ShapeDtypeStruct((1, 2048, 128), BF),
            jax.ShapeDtypeStruct((1, 2048, 128), BF),
        ),
        in_specs=[vmem] * 3,
        out_specs=(hbm, hbm, hbm),
        scratch_shapes=[dma((3,))],
    )(*[pltpu.with_memory_space_constraint(grad, pltpu.VMEM) for grad in grads])


def solution(mesh):
    return jax.shard_map(
        body,
        mesh=mesh,
        in_specs=(
            P("head", "ctx", None),
            P("head", "ctx", None),
            P("head", "ctx", None),
            P(("ctx", "head"), None),
            P(("ctx", "head"), None),
            P("head", "ctx"),
            P("ctx"),
        ),
        out_specs=(P("head", "ctx", None), P("head", "ctx", None), P("head", "ctx", None)),
        check_vma=False,
    )
```
